128 devices in a mesh: tm: 8 (over z, core), space: 16 (over y, x).
Axes of the slice: x: 4, y: 4, z: 4, core: 2. Of those that a mesh axis runs over, the one named last changes fastest.
Arguments:
- noise: bfloat16 [32, 1024, 8192], P('tm', 'space'), may hold values from -4 to 4
- scale: float32 [32, 8192], P('tm'), may hold values from 0.55 to 1
- tiles: bfloat16 [32, 64, 3, 128, 128], P('tm', 'space'), may hold values from -0.375 to 0.375
- columns: int32 [32, 64, 3], P('tm', 'space'), may hold values from 0 to 63, as said below
Outputs:
- samples: bfloat16 [32, 1024, 8192], P('tm', 'space')
The draws below stay inside these ranges and needn't reach their ends.
Inputs may be any that keep to these rules, and one draw needn't show every extreme that they name: `columns`: in every tile row r of a time step the 3 entries are different, and the first is r itself.
All inputs are finite; a program needn't handle non-finite values.
Results may differ from the reference program's by a relative error of at most 0.03.
Values may be sent and summed in bfloat16 or wider, within the bound.
No kernel may reach another device: no remote copies, remote signals or barrier semaphores. Data moves between devices by JAX's collectives and lax.ppermute only.
A program may use at most 128 MiB of HBM per device.

```python
import math
import jax
import jax.numpy as jnp
from jax import lax

NODES = 8192
TILE = 128
KT = 3
NT = 64
TIME = 32
R = 1024


def draw_columns(key, part):
    keys = jax.random.split(key, TIME * NT)

    def one_row(row_key):
        offsets = jax.random.permutation(row_key, NT - 1)[:KT - 1] + 1
        return jnp.concatenate([jnp.zeros((1,), jnp.int32), offsets.astype(jnp.int32)])
    offsets = jax.vmap(one_row)(keys).reshape(TIME, NT, KT)
    own_rows = jnp.arange(NT, dtype=jnp.int32)[None, :, None]
    return ((own_rows + offsets) % NT).astype(jnp.int32)


def steps_of(stream_key, dims, shards, smallest, largest):
    def one(dim, shards_of):
        heights = jax.random.uniform(jax.random.fold_in(jax.random.fold_in(stream_key, 6), dim), (shards_of,), jnp.float32, smallest / len(shards), largest / len(shards))
        return jnp.repeat(jnp.exp(heights), dims[dim] // shards_of).reshape((-1,) + (1,) * (len(dims) - dim - 1))

    gain = one(*shards[0])
    for cut in shards[1:]:
        gain = gain * one(*cut)
    return gain


def scatter_about(rng, shape, scale, limit, cuts=(), kind=jnp.bfloat16):
    entries = scale * jax.random.normal(rng, shape, jnp.float32)
    if cuts:
        entries = entries * steps_of(rng, shape, cuts, -0.22, 0.18)
    return jnp.clip(entries, -limit, limit).astype(kind)


def setup_inputs(seed: int = 0) -> dict:
    seeds = jax.random.split(jax.random.key(seed), 5)
    return {
        "noise": scatter_about(seeds[0], (TIME, R, NODES), 0.5, 4.0, ((0, 8), (1, 16))),
        "scale": jnp.clip(jnp.exp(math.log(1.0) - 0.597837 * jax.random.uniform(seeds[1], (TIME, NODES), jnp.float32) ** steps_of(seeds[1], (TIME, NODES), ((0, 8),), -0.2, 0.2)), 0.55, 1.0),
        "tiles": scatter_about(seeds[2], (TIME, NT, KT, TILE, TILE), (KT * TILE * 5 // 8) ** -0.5, 0.375, ((0, 8), (1, 16))),
        "columns": draw_columns(jax.random.fold_in(seeds[4], 71), 0),
    }


def reference(noise, scale, tiles, columns):
    sample_count = noise.shape[1]
    node_count = noise.shape[2]
    tile_rows = tiles.shape[1]
    tile_size = tiles.shape[3]

    def one_step(current, inputs):
        noise_step, scale_step, tile_step, column_step = inputs
        picked = current.reshape(sample_count, tile_rows, tile_size)[:, column_step]
        mixed = jnp.einsum("srkj,rkij->sri", picked.astype(jnp.float32), tile_step.astype(jnp.float32))
        updated = scale_step[None, :] * (noise_step.astype(jnp.float32) + mixed.reshape(sample_count, node_count))
        updated = updated.astype(jnp.bfloat16)
        return updated, updated

    start_field = jnp.zeros((sample_count, node_count), jnp.bfloat16)
    _, produced = lax.scan(one_step, start_field, (noise, scale, tiles, columns), reverse=True)
    return produced
```

```python
import functools
import jax
import jax.numpy as jnp
from jax import lax
from jax.experimental import pallas as pl
from jax.experimental.pallas import tpu as pltpu
from jax.sharding import PartitionSpec as P

BLOCKS = 2
GROUP = 16


def sweep_kernel(
    steps, rows, width, group, block,
    state, columns, tiles, noise, scale, front, _, out, front_out,
    tile_buf, noise_buf, *rest,
):
    fields = rest[:steps]
    tile_sem, noise_sem, out_sem = rest[steps:]
    size = tiles.shape[-1]
    kt = tiles.shape[2] // size
    groups = rows // group
    mine = pl.ds(block * width, width)

    def tile_copy(s, g):
        part = pl.ds(g * group, group)
        return pltpu.make_async_copy(tiles.at[s, part], tile_buf.at[s, part], tile_sem.at[s, g])

    def noise_copy(s):
        return pltpu.make_async_copy(noise.at[s, mine], noise_buf.at[s], noise_sem.at[s])

    def out_copy(s):
        return pltpu.make_async_copy(fields[s], out.at[s, mine], out_sem.at[s])

    @pl.when(state[0] == 1)
    def _active():
        for s in reversed(range(steps)):
            noise_copy(s).start()
            for g in range(groups):
                tile_copy(s, g).start()
        for s in reversed(range(steps)):
            source = front if s == steps - 1 else fields[s + 1]
            target = fields[s]
            noise_copy(s).wait()

            def one_group(g, carry):
                tile_copy(s, g).wait()
                picked = []
                for q in range(group):
                    r = g * group + q
                    picked.append([
                        source[:, pl.ds(pl.multiple_of(columns[(s * rows + r) * kt + k] * size, size), size)]
                        for k in range(kt)
                    ])
                mixed = [
                    jnp.dot(
                        jnp.concatenate(picked[q], axis=1),
                        tile_buf[s, g * group + q],
                        preferred_element_type=jnp.float32,
                    )
                    for q in range(group)
                ]
                for q in range(group):
                    lanes = pl.ds(pl.multiple_of((g * group + q) * size, size), size)
                    total = noise_buf[s, :, lanes].astype(jnp.float32) + mixed[q]
                    value = (scale[s : s + 1, lanes] * total).astype(jnp.bfloat16)
                    target[:, lanes] = value
                    if s == 0:
                        front_out[:, lanes] = value
                return carry

            lax.fori_loop(0, groups, one_group, 0)
            out_copy(s).start()
        for s in range(steps):
            out_copy(s).wait()


def sweep(state, columns, tiles, noise, scale, front, out, block, width):
    steps, rows = tiles.shape[:2]
    node_count = noise.shape[-1]
    group = min(GROUP, rows)
    groups = rows // group
    anywhere = pl.BlockSpec(memory_space=pl.ANY)
    smem = pl.BlockSpec(memory_space=pltpu.SMEM)
    vmem = pl.BlockSpec(memory_space=pltpu.VMEM)
    return pl.pallas_call(
        functools.partial(sweep_kernel, steps, rows, width, group, block),
        out_shape=(
            jax.ShapeDtypeStruct(out.shape, out.dtype),
            jax.ShapeDtypeStruct(front.shape, front.dtype),
        ),
        in_specs=[smem, smem, anywhere, anywhere, vmem, vmem, anywhere],
        out_specs=(anywhere, vmem),
        input_output_aliases={6: 0},
        scratch_shapes=[
            pltpu.VMEM(tiles.shape, jnp.bfloat16),
            pltpu.VMEM((steps, width, node_count), jnp.bfloat16),
            *[pltpu.VMEM((width, node_count), jnp.bfloat16) for _ in range(steps)],
            pltpu.SemaphoreType.DMA((steps, groups)),
            pltpu.SemaphoreType.DMA((steps,)),
            pltpu.SemaphoreType.DMA((steps,)),
        ],
        compiler_params=pltpu.CompilerParams(vmem_limit_bytes=56 << 20),
        name="sweep",
    )(state, columns, tiles, noise, scale, front, out)


def on_device(noise, scale, tiles, columns):
    steps, local_samples, node_count = noise.shape
    local_rows, kt, size = tiles.shape[1:4]
    parts = lax.axis_size("tm")
    me = lax.axis_index("tm")
    width = local_samples // BLOCKS
    turned = jnp.swapaxes(tiles, 3, 4).reshape(steps, local_rows, kt * size, size)
    full_tiles = lax.all_gather(turned, "space", axis=1, tiled=True)
    full_columns = lax.all_gather(columns, "space", axis=1, tiled=True).reshape(-1)

    out = jnp.zeros(noise.shape, jnp.bfloat16)
    fronts = [jnp.zeros((width, node_count), jnp.bfloat16) for _ in range(BLOCKS)]
    for part in reversed(range(parts)):
        state = (me == part).astype(jnp.int32).reshape(1)
        for block in range(BLOCKS):
            out, front = sweep(
                state, full_columns, full_tiles, noise, scale, fronts[block], out, block, width
            )
            if part > 0:
                fronts[block] = lax.ppermute(front, "tm", [(part, part - 1)])
    return out


def solution(mesh):
    placed = (
        P("tm", "space", None),
        P("tm", None),
        P("tm", "space", None, None, None),
        P("tm", "space", None),
    )
    return jax.shard_map(
        on_device, mesh=mesh, in_specs=placed, out_specs=P("tm", "space", None), check_vma=False
    )
```

```python
import functools
import jax
import jax.numpy as jnp
from jax import lax
from jax.experimental import pallas as pl
from jax.experimental.pallas import tpu as pltpu
from jax.sharding import PartitionSpec as P

BLOCKS = 2
GROUP = 32


def sweep_kernel(
    part, block, place, columns, tiles, noise, scale, front, _, out, front_out,
    out_buf, even, odd, out_sem,
):
    steps, rows, depth, size = tiles.shape
    kt = depth // size
    width = front.shape[1]
    group = min(GROUP, rows)
    mine = pl.ds(block * width, width)

    def out_copy(s):
        return pltpu.make_async_copy(out_buf.at[s], out.at[s, mine], out_sem.at[s])

    def one_step(s, source, target):
        def one_group(g, carry):
            picked = [
                jnp.concatenate(
                    [source[columns[(s * rows + g * group + q) * kt + k]] for k in range(kt)], axis=1
                )
                for q in range(group)
            ]
            mixed = [
                jnp.dot(picked[q], tiles[s, g * group + q], preferred_element_type=jnp.float32)
                for q in range(group)
            ]
            for q in range(group):
                r = g * group + q
                lanes = pl.ds(pl.multiple_of(r * size, size), size)
                total = noise[s, mine, lanes].astype(jnp.float32) + mixed[q]
                value = (scale[s, :, lanes] * total).astype(jnp.bfloat16)
                out_buf[s, :, lanes] = value
                target[r] = value
            return carry

        lax.fori_loop(0, rows // group, one_group, 0)
        out_copy(s).start()

    @pl.when(place[0] == part)
    def _active():
        even[...] = front[...]

        def two_steps(i, carry):
            s = steps - 1 - 2 * i
            one_step(s, even, odd)
            one_step(s - 1, odd, even)
            return carry

        lax.fori_loop(0, steps // 2, two_steps, 0)
        front_out[...] = even[...]
        for s in range(steps):
            out_copy(s).wait()


def sweep(place, columns, tiles, noise, scale, front, out, part, block):
    steps = tiles.shape[0]
    width = front.shape[1]
    node_count = noise.shape[-1]
    anywhere = pl.BlockSpec(memory_space=pl.ANY)
    smem = pl.BlockSpec(memory_space=pltpu.SMEM)
    vmem = pl.BlockSpec(memory_space=pltpu.VMEM)
    return pl.pallas_call(
        functools.partial(sweep_kernel, part, block),
        out_shape=(
            jax.ShapeDtypeStruct(out.shape, out.dtype),
            jax.ShapeDtypeStruct(front.shape, front.dtype),
        ),
        in_specs=[smem, smem, vmem, vmem, vmem, vmem, anywhere],
        out_specs=(anywhere, vmem),
        input_output_aliases={6: 0},
        scratch_shapes=[
            pltpu.VMEM((steps, width, node_count), jnp.bfloat16),
            pltpu.VMEM(front.shape, jnp.bfloat16),
            pltpu.VMEM(front.shape, jnp.bfloat16),
            pltpu.SemaphoreType.DMA((steps,)),
        ],
        compiler_params=pltpu.CompilerParams(vmem_limit_bytes=12 << 20),
        name="sweep",
    )(place, columns, tiles, noise, scale, front, out)


def on_device(noise, scale, tiles, columns):
    steps, local_samples, node_count = noise.shape
    local_rows, kt, size = tiles.shape[1:4]
    parts = lax.axis_size("tm")
    place = lax.axis_index("tm").astype(jnp.int32).reshape(1)
    width = local_samples // BLOCKS
    turned = jnp.swapaxes(tiles, 3, 4).reshape(steps, local_rows, kt * size, size)
    full_tiles = lax.all_gather(turned, "space", axis=1, tiled=True)
    full_columns = lax.all_gather(columns, "space", axis=1, tiled=True).reshape(-1)
    scale_rows = scale.reshape(steps, 1, node_count)

    out = jnp.zeros(noise.shape, jnp.bfloat16)
    fronts = [jnp.zeros((node_count // size, width, size), jnp.bfloat16) for _ in range(BLOCKS)]
    for part in reversed(range(parts)):
        for block in range(BLOCKS):
            out, front = sweep(
                place, full_columns, full_tiles, noise, scale_rows, fronts[block], out, part, block
            )
            if part > 0:
                fronts[block] = lax.ppermute(front, "tm", [(part, part - 1)])
    return out


def solution(mesh):
    placed = (
        P("tm", "space", None),
        P("tm", None),
        P("tm", "space", None, None, None),
        P("tm", "space", None),
    )
    return jax.shard_map(
        on_device, mesh=mesh, in_specs=placed, out_specs=P("tm", "space", None), check_vma=False
    )
```

```python
import functools
import jax
import jax.numpy as jnp
from jax import lax
from jax.experimental import pallas as pl
from jax.experimental.pallas import tpu as pltpu
from jax.sharding import PartitionSpec as P

BLOCKS = 2
GROUP = 6
SIDE = 4
PAD = 16
ENTRY = 16


def sweep_kernel(part, block, first, kt, local_rows, *refs):
    place, near_table, far_table, near, far, noise, scale = refs[:7]
    front = None if first else refs[7]
    out, front_out, out_buf, even, odd, out_sem = refs[-6:]
    steps, size = near.shape[1], near.shape[3]
    depth = kt * size
    width = even.shape[1]
    mine = pl.ds(block * width, width)

    def out_copy(s):
        return pltpu.make_async_copy(out_buf.at[s], out.at[s, mine], out_sem.at[s])

    def some_rows(s, table, tiles, start, count, source, target):
        row, picked, mixed = [], [], []
        for b in range(count):
            entry = ((start + b) * steps + s) * ENTRY
            for q in range(local_rows):
                row.append(table[entry + local_rows * kt] * local_rows + q)
                picked.append(
                    jnp.concatenate([source[table[entry + q * kt + k]] for k in range(kt)], axis=1)
                )
        for b in range(count):
            for q in range(local_rows):
                mixed.append(
                    jnp.dot(
                        picked[b * local_rows + q],
                        tiles[start + b, s, q * depth : (q + 1) * depth],
                        preferred_element_type=jnp.float32,
                    )
                )
        for r, value in zip(row, mixed):
            lanes = pl.ds(pl.multiple_of(r * size, size), size)
            total = noise[s, mine, lanes].astype(jnp.float32) + value
            value = (scale[s, :, lanes] * total).astype(jnp.bfloat16)
            out_buf[s, :, lanes] = value
            target[r] = value

    def one_step(s, source, target):
        def one_group(g, carry):
            some_rows(s, near_table, near, g * GROUP, GROUP, source, target)
            return carry

        lax.fori_loop(0, near.shape[0] // GROUP, one_group, 0)
        some_rows(s, far_table, far, 0, far.shape[0], source, target)
        out_copy(s).start()

    @pl.when(place[0] == part)
    def _active():
        even[...] = jnp.zeros(even.shape, even.dtype) if first else front[...]

        def two_steps(i, carry):
            s = steps - 1 - 2 * i
            one_step(s, even, odd)
            one_step(s - 1, odd, even)
            return carry

        lax.fori_loop(0, steps // 2, two_steps, 0)
        front_out[...] = even[...]
        for s in range(steps):
            out_copy(s).wait()


def sweep(place, tables, tiles, noise, scale, front, out, part, block, kt, local_rows):
    steps, size = tiles[0].shape[1], tiles[0].shape[3]
    node_count = noise.shape[-1]
    width = noise.shape[1] // BLOCKS
    field = jax.ShapeDtypeStruct((node_count // size, width, size), jnp.bfloat16)
    anywhere = pl.BlockSpec(memory_space=pl.ANY)
    smem = pl.BlockSpec(memory_space=pltpu.SMEM)
    vmem = pl.BlockSpec(memory_space=pltpu.VMEM)
    more = [] if front is None else [front]
    specs = [smem, smem, smem, vmem, vmem, vmem, vmem] + [vmem] * len(more)
    aliases = {}
    if out is not None:
        aliases = {len(specs): 0}
        specs.append(anywhere)
        more.append(out)
    return pl.pallas_call(
        functools.partial(sweep_kernel, part, block, front is None, kt, local_rows),
        out_shape=(jax.ShapeDtypeStruct(noise.shape, noise.dtype), field),
        in_specs=specs,
        out_specs=(anywhere, vmem),
        input_output_aliases=aliases,
        scratch_shapes=[
            pltpu.VMEM((steps, width, node_count), jnp.bfloat16),
            pltpu.VMEM(field.shape, jnp.bfloat16),
            pltpu.VMEM(field.shape, jnp.bfloat16),
            pltpu.SemaphoreType.DMA((steps,)),
        ],
        compiler_params=pltpu.CompilerParams(vmem_limit_bytes=12 << 20),
        name="sweep",
    )(place, *tables, *tiles, noise, scale, *more)


def assemble_kernel(places, *refs):
    count = len(places)
    pieces, (target, table), held, (come, go) = refs[:count], refs[count : count + 2], refs[count + 2 : -2], refs[-2:]
    into = [pltpu.make_async_copy(pieces[i], held[i], come.at[i]) for i in range(count)]
    back = [
        pltpu.make_async_copy(
            held[i], target.at[pl.ds(q, held[i].shape[0]), pl.ds(s, held[i].shape[1])], go.at[i]
        )
        for i, (q, s) in enumerate(places)
    ]
    for copy in into:
        copy.start()
    for i in range(count):
        into[i].wait()
        back[i].start()
    steps, span, size = target.shape[1:]
    per_line = size // ENTRY
    where = {}
    for i, (q, s) in enumerate(places):
        for b in range(held[i].shape[0]):
            for t in range(held[i].shape[1]):
                where[(q + b) * steps + s + t] = held[i], b, t
    for line in range(len(where) // per_line):
        value = jnp.zeros((1, size), jnp.float32)
        for j in range(per_line):
            buffer, b, t = where[line * per_line + j]
            entries = jnp.sum(buffer[b, t, span - PAD :].astype(jnp.float32), axis=0, keepdims=True)
            value = value + (pltpu.roll(entries, j * ENTRY, 1) if j else entries)
        table[pl.ds(line, 1)] = value.astype(jnp.int32)
    for copy in back:
        copy.wait()


def assemble(pieces, places, blocks, steps):
    anywhere = pl.BlockSpec(memory_space=pl.ANY)
    span, size = pieces[0].shape[2:]
    bytes_moved = sum(p.size * 4 for p in pieces)
    tiles, table = pl.pallas_call(
        functools.partial(assemble_kernel, places),
        out_shape=(
            jax.ShapeDtypeStruct((blocks, steps, span, size), jnp.bfloat16),
            jax.ShapeDtypeStruct((blocks * steps * ENTRY // size, size), jnp.int32),
        ),
        in_specs=[anywhere] * len(pieces),
        out_specs=(anywhere, pl.BlockSpec(memory_space=pltpu.VMEM)),
        scratch_shapes=[pltpu.VMEM(p.shape, p.dtype) for p in pieces]
        + [pltpu.SemaphoreType.DMA((len(pieces),))] * 2,
        compiler_params=pltpu.CompilerParams(vmem_limit_bytes=bytes_moved // 2 + (1 << 20)),
        cost_estimate=pl.CostEstimate(flops=0, bytes_accessed=bytes_moved, transcendentals=0),
        name="assemble",
    )(*pieces)
    return tiles, table.reshape(-1)


def moved(value, dx, dy):
    pairs = [
        (y * SIDE + x, (y + dy) % SIDE * SIDE + (x + dx) % SIDE) for y in range(SIDE) for x in range(SIDE)
    ]
    return lax.ppermute(value, "space", pairs)


def along(axis, by):
    return (by, 0) if axis == 0 else (0, by)


def ring_gather(block, first, second):
    low = moved(block, *along(first, 1))
    high = moved(block, *along(first, -1))
    far_low = moved(low[:, :1], *along(first, 1))
    far_high = moved(high[:, 1:], *along(first, -1))
    far = jnp.concatenate([far_low, far_high], axis=1)
    bundle = jnp.concatenate([block, low, high, far], axis=0)
    half = bundle.shape[0] // 2
    below = moved(bundle, *along(second, 1))
    above = moved(bundle, *along(second, -1))
    far_below = moved(below[:half], *along(second, 1))
    far_above = moved(above[half:], *along(second, -1))
    return (bundle, below, above), (far_below, far_above)


def on_device(noise, scale, tiles, columns):
    steps, local_samples, node_count = noise.shape
    local_rows, kt, size = tiles.shape[1:4]
    parts = lax.axis_size("tm")
    place = lax.axis_index("tm").astype(jnp.int32).reshape(1)
    spot = lax.axis_index("space").astype(jnp.int32)
    half = steps // 2
    scale_rows = scale.reshape(steps, 1, node_count)

    span = local_rows * kt * size + PAD
    turned = jnp.swapaxes(tiles, 3, 4).reshape(steps, span - PAD, size)
    entries = jnp.concatenate(
        [columns.reshape(steps, local_rows * kt), jnp.broadcast_to(spot, (steps, 1))], axis=1
    ).astype(jnp.bfloat16)
    entries = jnp.pad(entries[:, None], ((0, 0), (0, PAD - 1), (0, size - entries.shape[1])))
    block = jnp.concatenate([turned, entries], axis=1)[None]

    late_near, late_far = ring_gather(block[:, half:], 0, 1)
    early_near, early_far = ring_gather(block[:, :half], 1, 0)
    near, near_table = assemble(
        (*late_near, *early_near), [(i * SIDE, s) for s in (half, 0) for i in range(3)], 3 * SIDE, steps
    )
    far, far_table = assemble(
        (*late_far, *early_far), [(i * SIDE // 2, s) for s in (half, 0) for i in range(2)], SIDE, steps
    )
    tables, full = (near_table, far_table), (near, far)

    out = None
    fronts = [None] * BLOCKS
    for part in reversed(range(parts)):
        for block in range(BLOCKS):
            out, front = sweep(
                place, tables, full, noise, scale_rows, fronts[block], out, part, block, kt, local_rows
            )
            if part > 0:
                fronts[block] = lax.ppermute(front, "tm", [(part, part - 1)])
    return out


def solution(mesh):
    placed = (
        P("tm", "space", None),
        P("tm", None),
        P("tm", "space", None, None, None),
        P("tm", "space", None),
    )
    return jax.shard_map(
        on_device, mesh=mesh, in_specs=placed, out_specs=P("tm", "space", None), check_vma=False
    )
```

```python
import functools
import jax
import jax.numpy as jnp
from jax import lax
from jax.experimental import pallas as pl
from jax.experimental.pallas import tpu as pltpu
from jax.sharding import PartitionSpec as P

BLOCKS = 2
SIDE = 4
PAD = 16
ENTRY = 16


def sweep_kernel(part, block, first, kt, local_rows, *refs):
    place, near_table, far_table, near, far, noise, scale = refs[:7]
    front = None if first else refs[7]
    out, front_out, out_buf, even, odd, out_sem = refs[-6:]
    steps, size = near.shape[1], near.shape[3]
    depth = kt * size
    width = even.shape[1]
    mine = pl.ds(block * width, width)

    def out_copy(s):
        return pltpu.make_async_copy(out_buf.at[s], out.at[s, mine], out_sem.at[s])

    def one_step(i, carry):
        s = steps - 1 - i
        row, picked, weight = [], [], []
        for table, tiles in ((near_table, near), (far_table, far)):
            for b in range(tiles.shape[0]):
                entry = (b * steps + s) * ENTRY
                for q in range(local_rows):
                    row.append(table[entry + local_rows * kt] * local_rows + q)
                    picked.append([even[table[entry + q * kt + k]] for k in range(kt)])
                    weight.append((tiles, b, q * depth))
        zero = jnp.zeros((width, size), jnp.bfloat16)

        def part_of(r, start, stop):
            tiles, b, base = weight[r]
            return tiles[b, s, base + start : base + stop]

        def product(left, right):
            return jnp.dot(left, right, preferred_element_type=jnp.float32)

        mixed = [None] * len(row)
        for r in range(0, len(row), 2):
            main = [
                product(jnp.concatenate(picked[r + j][:-1], axis=1), part_of(r + j, 0, depth - size))
                for j in range(2)
            ]
            last = product(
                jnp.concatenate(
                    [
                        jnp.concatenate([picked[r][-1], zero], axis=1),
                        jnp.concatenate([zero, picked[r + 1][-1]], axis=1),
                    ],
                    axis=0,
                ),
                jnp.concatenate([part_of(r, depth - size, depth), part_of(r + 1, depth - size, depth)], axis=0),
            )
            mixed[r] = main[0] + last[:width]
            mixed[r + 1] = main[1] + last[width:]
        for r, value in zip(row, mixed):
            lanes = pl.ds(pl.multiple_of(r * size, size), size)
            total = noise[s, mine, lanes].astype(jnp.float32) + value
            value = (scale[s, :, lanes] * total).astype(jnp.bfloat16)
            out_buf[s, :, lanes] = value
            odd[r] = value
        out_copy(s).start()
        even[...] = odd[...]
        return carry

    @pl.when(place[0] == part)
    def _active():
        even[...] = jnp.zeros(even.shape, even.dtype) if first else front[...]
        lax.fori_loop(0, steps, one_step, 0)
        front_out[...] = even[...]
        for s in range(steps):
            out_copy(s).wait()


def sweep(place, tables, tiles, noise, scale, front, out, part, block, kt, local_rows):
    steps, size = tiles[0].shape[1], tiles[0].shape[3]
    node_count = noise.shape[-1]
    width = noise.shape[1] // BLOCKS
    field = jax.ShapeDtypeStruct((node_count // size, width, size), jnp.bfloat16)
    anywhere = pl.BlockSpec(memory_space=pl.ANY)
    smem = pl.BlockSpec(memory_space=pltpu.SMEM)
    vmem = pl.BlockSpec(memory_space=pltpu.VMEM)
    more = [] if front is None else [front]
    specs = [smem, smem, smem, vmem, vmem, vmem, vmem] + [vmem] * len(more)
    aliases = {}
    if out is not None:
        aliases = {len(specs): 0}
        specs.append(anywhere)
        more.append(out)
    return pl.pallas_call(
        functools.partial(sweep_kernel, part, block, front is None, kt, local_rows),
        out_shape=(jax.ShapeDtypeStruct(noise.shape, noise.dtype), field),
        in_specs=specs,
        out_specs=(anywhere, vmem),
        input_output_aliases=aliases,
        scratch_shapes=[
            pltpu.VMEM((steps, width, node_count), jnp.bfloat16),
            pltpu.VMEM(field.shape, jnp.bfloat16),
            pltpu.VMEM(field.shape, jnp.bfloat16),
            pltpu.SemaphoreType.DMA((steps,)),
        ],
        compiler_params=pltpu.CompilerParams(vmem_limit_bytes=12 << 20),
        name="sweep",
    )(place, *tables, *tiles, noise, scale, *more)


def assemble_kernel(places, *refs):
    count = len(places)
    pieces, (target, table), pads, sems = refs[:count], refs[count : count + 2], refs[count + 2 : -1], refs[-1]
    steps, span, size = target.shape[1:]
    copies = []
    for i, (q, s) in enumerate(places):
        blocks, some = pieces[i].shape[:2]
        copies.append(pltpu.make_async_copy(pieces[i].at[:, :, pl.ds(span - PAD, PAD)], pads[i], sems.at[i, 0]))
        copies.append(
            pltpu.make_async_copy(pieces[i], target.at[pl.ds(q, blocks), pl.ds(s, some)], sems.at[i, 1])
        )
    for copy in copies:
        copy.start()
    for copy in copies[::2]:
        copy.wait()
    per_line = size // ENTRY
    where = {}
    for i, (q, s) in enumerate(places):
        for b in range(pads[i].shape[0]):
            for t in range(pads[i].shape[1]):
                where[(q + b) * steps + s + t] = pads[i], b, t
    for line in range(len(where) // per_line):
        value = jnp.zeros((1, size), jnp.float32)
        for j in range(per_line):
            buffer, b, t = where[line * per_line + j]
            entries = jnp.sum(buffer[b, t].astype(jnp.float32), axis=0, keepdims=True)
            value = value + (pltpu.roll(entries, j * ENTRY, 1) if j else entries)
        table[pl.ds(line, 1)] = value.astype(jnp.int32)
    for copy in copies[1::2]:
        copy.wait()


def assemble(pieces, places, blocks, steps):
    anywhere = pl.BlockSpec(memory_space=pl.ANY)
    span, size = pieces[0].shape[2:]
    bytes_moved = sum(p.size * 4 for p in pieces)
    tiles, table = pl.pallas_call(
        functools.partial(assemble_kernel, places),
        out_shape=(
            jax.ShapeDtypeStruct((blocks, steps, span, size), jnp.bfloat16),
            jax.ShapeDtypeStruct((blocks * steps * ENTRY // size, size), jnp.int32),
        ),
        in_specs=[anywhere] * len(pieces),
        out_specs=(anywhere, pl.BlockSpec(memory_space=pltpu.VMEM)),
        scratch_shapes=[pltpu.VMEM((*p.shape[:2], PAD, size), p.dtype) for p in pieces]
        + [pltpu.SemaphoreType.DMA((len(pieces), 2))],
        compiler_params=pltpu.CompilerParams(vmem_limit_bytes=2 << 20),
        cost_estimate=pl.CostEstimate(flops=0, bytes_accessed=bytes_moved, transcendentals=0),
        name="assemble",
    )(*pieces)
    return tiles, table.reshape(-1)


def moved(value, dx, dy):
    pairs = [
        (y * SIDE + x, (y + dy) % SIDE * SIDE + (x + dx) % SIDE) for y in range(SIDE) for x in range(SIDE)
    ]
    return lax.ppermute(value, "space", pairs)


def along(axis, by):
    return (by, 0) if axis == 0 else (0, by)


def ring_gather(block, first, second):
    low = moved(block, *along(first, 1))
    high = moved(block, *along(first, -1))
    far_low = moved(low[:, :1], *along(first, 1))
    far_high = moved(high[:, 1:], *along(first, -1))
    far = jnp.concatenate([far_low, far_high], axis=1)
    bundle = jnp.concatenate([block, low, high, far], axis=0)
    half = bundle.shape[0] // 2
    below = moved(bundle, *along(second, 1))
    above = moved(bundle, *along(second, -1))
    far_below = moved(below[:half], *along(second, 1))
    far_above = moved(above[half:], *along(second, -1))
    return (bundle, below, above), (far_below, far_above)


def on_device(noise, scale, tiles, columns):
    steps, local_samples, node_count = noise.shape
    local_rows, kt, size = tiles.shape[1:4]
    parts = lax.axis_size("tm")
    place = lax.axis_index("tm").astype(jnp.int32).reshape(1)
    spot = lax.axis_index("space").astype(jnp.int32)
    half = steps // 2
    scale_rows = scale.reshape(steps, 1, node_count)

    span = local_rows * kt * size + PAD
    turned = jnp.swapaxes(tiles, 3, 4).reshape(steps, span - PAD, size)
    entries = jnp.concatenate(
        [columns.reshape(steps, local_rows * kt), jnp.broadcast_to(spot, (steps, 1))], axis=1
    ).astype(jnp.bfloat16)
    entries = jnp.pad(entries[:, None], ((0, 0), (0, PAD - 1), (0, size - entries.shape[1])))
    block = jnp.concatenate([turned, entries], axis=1)[None]

    late_near, late_far = ring_gather(block[:, half:], 0, 1)
    early_near, early_far = ring_gather(block[:, :half], 1, 0)
    near, near_table = assemble(
        [pltpu.with_memory_space_constraint(p, pltpu.HBM) for p in (*late_near, *early_near)],
        [(i * SIDE, s) for s in (half, 0) for i in range(3)],
        3 * SIDE,
        steps,
    )
    far, far_table = assemble(
        (*late_far, *early_far), [(i * SIDE // 2, s) for s in (half, 0) for i in range(2)], SIDE, steps
    )
    tables, full = (near_table, far_table), (near, far)

    out = None
    fronts = [None] * BLOCKS
    for part in reversed(range(parts)):
        for block in range(BLOCKS):
            out, front = sweep(
                place, tables, full, noise, scale_rows, fronts[block], out, part, block, kt, local_rows
            )
            if part > 0:
                fronts[block] = lax.ppermute(front, "tm", [(part, part - 1)])
    return out


def solution(mesh):
    placed = (
        P("tm", "space", None),
        P("tm", None),
        P("tm", "space", None, None, None),
        P("tm", "space", None),
    )
    return jax.shard_map(
        on_device, mesh=mesh, in_specs=placed, out_specs=P("tm", "space", None), check_vma=False
    )
```

```python
import functools
import jax
import jax.numpy as jnp
from jax import lax
from jax.experimental import pallas as pl
from jax.experimental.pallas import tpu as pltpu
from jax.sharding import PartitionSpec as P

BLOCKS = 2
SIDE = 4
PAD = 16
ENTRY = 16


def sweep_kernel(part, block, before, first, ends, kt, local_rows, *refs):
    table, near, far, noise, scale = refs[:5]
    refs = list(refs[5:])
    front = None if first else refs.pop(0)
    tail = None if before is None else refs.pop(0)
    if before is not None:
        refs.pop(0)
    out = refs.pop(0)
    front_out, tail_out = (None, None) if ends else (refs.pop(0), None)
    if not (part == 0 and block == BLOCKS - 1):
        tail_out = refs.pop(0)
    out_buf, even, odd, out_sem, tail_sem = refs
    steps, size = near.shape[1], near.shape[3]
    depth = kt * size
    width = even.shape[1]
    mine = pl.ds(block * width, width)
    here = table[local_rows * kt + 1]

    def out_copy(s):
        return pltpu.make_async_copy(out_buf.at[s], out.at[s, mine], out_sem.at[s])

    def flush(action):
        if before is not None:
            held = pl.ds(before[1] * width, width)

            @pl.when(here == before[0])
            def _flush():
                action(pltpu.make_async_copy(tail, out.at[0, held], tail_sem.at[0]))

    def one_step(i, carry):
        s = steps - 1 - i
        row, picked, weight = [], [], []
        for base, tiles in ((0, near), (near.shape[0], far)):
            for b in range(tiles.shape[0]):
                entry = ((base + b) * steps + s) * ENTRY
                for q in range(local_rows):
                    row.append(table[entry + local_rows * kt] * local_rows + q)
                    picked.append([even[table[entry + q * kt + k]] for k in range(kt)])
                    weight.append((tiles, b, q * depth))
        zero = jnp.zeros((width, size), jnp.bfloat16)

        def part_of(r, start, stop):
            tiles, b, base = weight[r]
            return tiles[b, s, base + start : base + stop]

        def product(left, right):
            return jnp.dot(left, right, preferred_element_type=jnp.float32)

        mixed = [None] * len(row)
        for r in range(0, len(row), 2):
            main = [
                product(jnp.concatenate(picked[r + j][:-1], axis=1), part_of(r + j, 0, depth - size))
                for j in range(2)
            ]
            last = product(
                jnp.concatenate(
                    [
                        jnp.concatenate([picked[r][-1], zero], axis=1),
                        jnp.concatenate([zero, picked[r + 1][-1]], axis=1),
                    ],
                    axis=0,
                ),
                jnp.concatenate([part_of(r, depth - size, depth), part_of(r + 1, depth - size, depth)], axis=0),
            )
            mixed[r] = main[0] + last[:width]
            mixed[r + 1] = main[1] + last[width:]
        for r, value in zip(row, mixed):
            lanes = pl.ds(pl.multiple_of(r * size, size), size)
            total = noise[s, mine, lanes].astype(jnp.float32) + value
            value = (scale[s, :, lanes] * total).astype(jnp.bfloat16)
            out_buf[s, :, lanes] = value
            odd[r] = value

        @pl.when(i < steps - 1)
        def _next():
            out_copy(s).start()
            even[...] = odd[...]

        return carry

    flush(lambda copy: copy.start())

    @pl.when(here == part)
    def _active():
        even[...] = jnp.zeros(even.shape, even.dtype) if first else front[...]
        lax.fori_loop(0, steps, one_step, 0)
        if front_out is not None:
            front_out[...] = odd[...]
        if tail_out is None:
            out_copy(0).start()
            out_copy(0).wait()
        else:
            tail_out[...] = out_buf[0]
        for s in range(1, steps):
            out_copy(s).wait()

    flush(lambda copy: copy.wait())


def sweep(table, tiles, noise, scale, front, tail, out, part, block, before, kt, local_rows):
    steps, size = tiles[0].shape[1], tiles[0].shape[3]
    node_count = noise.shape[-1]
    width = noise.shape[1] // BLOCKS
    field = jax.ShapeDtypeStruct((node_count // size, width, size), jnp.bfloat16)
    anywhere = pl.BlockSpec(memory_space=pl.ANY)
    smem = pl.BlockSpec(memory_space=pltpu.SMEM)
    vmem = pl.BlockSpec(memory_space=pltpu.VMEM)
    more = [value for value in (front, tail) if value is not None]
    specs = [smem, vmem, vmem, vmem, vmem] + [vmem] * len(more)
    aliases = {}
    if out is not None:
        aliases = {len(specs): 0}
        specs.append(anywhere)
        more.append(out)
    shapes, places = [jax.ShapeDtypeStruct(noise.shape, noise.dtype)], [anywhere]
    if part > 0:
        shapes.append(field)
        places.append(vmem)
    if part > 0 or block < BLOCKS - 1:
        shapes.append(jax.ShapeDtypeStruct((width, node_count), jnp.bfloat16))
        places.append(vmem)
    results = pl.pallas_call(
        functools.partial(sweep_kernel, part, block, before, front is None, part == 0, kt, local_rows),
        out_shape=tuple(shapes),
        in_specs=specs,
        out_specs=tuple(places),
        input_output_aliases=aliases,
        scratch_shapes=[
            pltpu.VMEM((steps, width, node_count), jnp.bfloat16),
            pltpu.VMEM(field.shape, jnp.bfloat16),
            pltpu.VMEM(field.shape, jnp.bfloat16),
            pltpu.SemaphoreType.DMA((steps,)),
            pltpu.SemaphoreType.DMA((1,)),
        ],
        compiler_params=pltpu.CompilerParams(vmem_limit_bytes=12 << 20),
        name="sweep",
    )(table, *tiles, noise, scale, *more)
    results = list(results)
    out = results.pop(0)
    front = results.pop(0) if part > 0 else None
    return out, front, results.pop(0) if results else None


def assemble_kernel(places, *refs):
    count = len(places)
    sems, pads = refs[-1], refs[-1 - count : -1]
    pieces, earlier, (target, table) = refs[:count], refs[count : -3 - count], refs[-3 - count : -1 - count]
    steps, span, size = target.shape[1:]
    copies = []
    for i, (q, s) in enumerate(places):
        blocks, some = pieces[i].shape[:2]
        copies.append(pltpu.make_async_copy(pieces[i].at[:, :, pl.ds(span - PAD, PAD)], pads[i], sems.at[i, 0]))
        copies.append(
            pltpu.make_async_copy(pieces[i], target.at[pl.ds(q, blocks), pl.ds(s, some)], sems.at[i, 1])
        )
    for copy in copies:
        copy.start()
    for copy in copies[::2]:
        copy.wait()
    per_line = size // ENTRY
    skip = earlier[0].shape[0] if earlier else 0
    if earlier:
        table[pl.ds(0, skip)] = earlier[0][...]
    where = {}
    for i, (q, s) in enumerate(places):
        for b in range(pads[i].shape[0]):
            for t in range(pads[i].shape[1]):
                where[(q + b) * steps + s + t] = pads[i], b, t
    for line in range(len(where) // per_line):
        value = jnp.zeros((1, size), jnp.float32)
        for j in range(per_line):
            buffer, b, t = where[line * per_line + j]
            entries = jnp.sum(buffer[b, t].astype(jnp.float32), axis=0, keepdims=True)
            value = value + (pltpu.roll(entries, j * ENTRY, 1) if j else entries)
        table[pl.ds(skip + line, 1)] = value.astype(jnp.int32)
    for copy in copies[1::2]:
        copy.wait()


def assemble(pieces, places, blocks, steps, earlier=()):
    anywhere = pl.BlockSpec(memory_space=pl.ANY)
    span, size = pieces[0].shape[2:]
    bytes_moved = sum(p.size * 4 for p in pieces)
    lines = blocks * steps * ENTRY // size + sum(e.shape[0] for e in earlier)
    vmem = pl.BlockSpec(memory_space=pltpu.VMEM)
    return pl.pallas_call(
        functools.partial(assemble_kernel, places),
        out_shape=(
            jax.ShapeDtypeStruct((blocks, steps, span, size), jnp.bfloat16),
            jax.ShapeDtypeStruct((lines, size), jnp.int32),
        ),
        in_specs=[anywhere] * len(pieces) + [vmem] * len(earlier),
        out_specs=(anywhere, vmem),
        scratch_shapes=[pltpu.VMEM((*p.shape[:2], PAD, size), p.dtype) for p in pieces]
        + [pltpu.SemaphoreType.DMA((len(pieces), 2))],
        compiler_params=pltpu.CompilerParams(vmem_limit_bytes=2 << 20),
        cost_estimate=pl.CostEstimate(flops=0, bytes_accessed=bytes_moved, transcendentals=0),
        name="assemble",
    )(*pieces, *earlier)


def moved(value, dx, dy):
    pairs = [
        (y * SIDE + x, (y + dy) % SIDE * SIDE + (x + dx) % SIDE) for y in range(SIDE) for x in range(SIDE)
    ]
    return lax.ppermute(value, "space", pairs)


def along(axis, by):
    return (by, 0) if axis == 0 else (0, by)


def ring_gather(block, first, second):
    low = moved(block, *along(first, 1))
    high = moved(block, *along(first, -1))
    far_low = moved(low[:, :1], *along(first, 1))
    far_high = moved(high[:, 1:], *along(first, -1))
    far = jnp.concatenate([far_low, far_high], axis=1)
    bundle = jnp.concatenate([block, low, high, far], axis=0)
    half = bundle.shape[0] // 2
    below = moved(bundle, *along(second, 1))
    above = moved(bundle, *along(second, -1))
    far_below = moved(below[:half], *along(second, 1))
    far_above = moved(above[half:], *along(second, -1))
    return (bundle, below, above), (far_below, far_above)


def on_device(noise, scale, tiles, columns):
    steps, local_samples, node_count = noise.shape
    local_rows, kt, size = tiles.shape[1:4]
    parts = lax.axis_size("tm")
    spot = jnp.stack([lax.axis_index("space"), lax.axis_index("tm")]).astype(jnp.int32)
    half = steps // 2
    scale_rows = scale.reshape(steps, 1, node_count)

    span = local_rows * kt * size + PAD
    turned = jnp.swapaxes(tiles, 3, 4).reshape(steps, span - PAD, size)
    entries = jnp.concatenate(
        [columns.reshape(steps, local_rows * kt), jnp.broadcast_to(spot, (steps, 2))], axis=1
    ).astype(jnp.bfloat16)
    entries = jnp.pad(entries[:, None], ((0, 0), (0, PAD - 1), (0, size - entries.shape[1])))
    block = jnp.concatenate([turned, entries], axis=1)[None]

    late_near, late_far = ring_gather(block[:, half:], 0, 1)
    early_near, early_far = ring_gather(block[:, :half], 1, 0)
    near, near_table = assemble(
        [pltpu.with_memory_space_constraint(p, pltpu.HBM) for p in (*late_near, *early_near)],
        [(i * SIDE, s) for s in (half, 0) for i in range(3)],
        3 * SIDE,
        steps,
    )
    far, table = assemble(
        (*late_far, *early_far),
        [(i * SIDE // 2, s) for s in (half, 0) for i in range(2)],
        SIDE,
        steps,
        (near_table,),
    )
    table, full = table.reshape(-1), (near, far)

    out = tail = before = None
    fronts = [None] * BLOCKS
    for part in reversed(range(parts)):
        for block in range(BLOCKS):
            out, front, tail = sweep(
                table, full, noise, scale_rows, fronts[block], tail, out, part, block, before, kt, local_rows
            )
            before = (part, block)
            if part > 0:
                fronts[block] = lax.ppermute(front, "tm", [(part, part - 1)])
    return out


def solution(mesh):
    placed = (
        P("tm", "space", None),
        P("tm", None),
        P("tm", "space", None, None, None),
        P("tm", "space", None),
    )
    return jax.shard_map(
        on_device, mesh=mesh, in_specs=placed, out_specs=P("tm", "space", None), check_vma=False
    )
```

```python
import functools
import jax
import jax.numpy as jnp
from jax import lax
from jax.experimental import pallas as pl
from jax.experimental.pallas import tpu as pltpu
from jax.sharding import PartitionSpec as P

BLOCKS = 2
SIDE = 4
PAD = 16
ENTRY = 16


def sweep_kernel(part, block, before, first, ends, kt, local_rows, *refs):
    table, near, far, noise, scale = refs[:5]
    refs = list(refs[5:])
    front = None if first else refs.pop(0)
    tail = None if before is None else refs.pop(0)
    if before is not None:
        refs.pop(0)
    out = refs.pop(0)
    front_out, tail_out = (None, None) if ends else (refs.pop(0), None)
    if not (part == 0 and block == BLOCKS - 1):
        tail_out = refs.pop(0)
    out_buf, even, odd, out_sem, tail_sem = refs
    steps, size = near.shape[1], near.shape[3]
    depth = kt * size
    width = even.shape[1]
    mine = pl.ds(block * width, width)
    here = table[local_rows * kt + 1]

    def out_copy(s):
        return pltpu.make_async_copy(out_buf.at[s], out.at[s, mine], out_sem.at[s])

    def flush(action):
        if before is not None:
            held = pl.ds(before[1] * width, width)

            @pl.when(here == before[0])
            def _flush():
                action(pltpu.make_async_copy(tail, out.at[0, held], tail_sem.at[0]))

    def one_step(i, carry):
        s = steps - 1 - i
        row, picked, weight = [], [], []
        for base, tiles in ((0, near), (near.shape[0], far)):
            for b in range(tiles.shape[0]):
                entry = ((base + b) * steps + s) * ENTRY
                for q in range(local_rows):
                    row.append(table[entry + local_rows * kt] * local_rows + q)
                    picked.append([even[table[entry + q * kt + k]] for k in range(kt)])
                    weight.append((tiles, b, q * depth))
        zero = jnp.zeros((width, size), jnp.bfloat16)

        def part_of(r, start, stop):
            tiles, b, base = weight[r]
            return tiles[b, s, base + start : base + stop]

        def product(left, right):
            return jnp.dot(left, right, preferred_element_type=jnp.float32)

        mixed = [None] * len(row)
        for r in range(0, len(row), 2):
            main = [
                product(jnp.concatenate(picked[r + j][:-1], axis=1), part_of(r + j, 0, depth - size))
                for j in range(2)
            ]
            last = product(
                jnp.concatenate(
                    [
                        jnp.concatenate([picked[r][-1], zero], axis=1),
                        jnp.concatenate([zero, picked[r + 1][-1]], axis=1),
                    ],
                    axis=0,
                ),
                jnp.concatenate([part_of(r, depth - size, depth), part_of(r + 1, depth - size, depth)], axis=0),
            )
            mixed[r] = main[0] + last[:width]
            mixed[r + 1] = main[1] + last[width:]
        for r, value in zip(row, mixed):
            lanes = pl.ds(pl.multiple_of(r * size, size), size)
            total = noise[s, mine, lanes].astype(jnp.float32) + value
            value = (scale[s, :, lanes] * total).astype(jnp.bfloat16)
            out_buf[s, :, lanes] = value
            odd[r] = value

        @pl.when(i < steps - 1)
        def _next():
            out_copy(s).start()
            even[...] = odd[...]

        return carry

    flush(lambda copy: copy.start())

    @pl.when(here == part)
    def _active():
        even[...] = jnp.zeros(even.shape, even.dtype) if first else front[...]
        lax.fori_loop(0, steps, one_step, 0)
        if front_out is not None:
            front_out[...] = odd[...]
        if tail_out is None:
            out_copy(0).start()
            out_copy(0).wait()
        else:
            tail_out[...] = out_buf[0]
        for s in range(1, steps):
            out_copy(s).wait()

    flush(lambda copy: copy.wait())


def sweep(table, tiles, noise, scale, front, tail, out, part, block, before, kt, local_rows):
    steps, size = tiles[0].shape[1], tiles[0].shape[3]
    node_count = noise.shape[-1]
    width = noise.shape[1] // BLOCKS
    field = jax.ShapeDtypeStruct((node_count // size, width, size), jnp.bfloat16)
    anywhere = pl.BlockSpec(memory_space=pl.ANY)
    smem = pl.BlockSpec(memory_space=pltpu.SMEM)
    vmem = pl.BlockSpec(memory_space=pltpu.VMEM)
    more = [value for value in (front, tail) if value is not None]
    specs = [smem, vmem, vmem, vmem, vmem] + [vmem] * len(more)
    aliases = {}
    if out is not None:
        aliases = {len(specs): 0}
        specs.append(anywhere)
        more.append(out)
    shapes, places = [jax.ShapeDtypeStruct(noise.shape, noise.dtype)], [anywhere]
    if part > 0:
        shapes.append(field)
        places.append(vmem)
    if part > 0 or block < BLOCKS - 1:
        shapes.append(jax.ShapeDtypeStruct((width, node_count), jnp.bfloat16))
        places.append(vmem)
    results = pl.pallas_call(
        functools.partial(sweep_kernel, part, block, before, front is None, part == 0, kt, local_rows),
        out_shape=tuple(shapes),
        in_specs=specs,
        out_specs=tuple(places),
        input_output_aliases=aliases,
        scratch_shapes=[
            pltpu.VMEM((steps, width, node_count), jnp.bfloat16),
            pltpu.VMEM(field.shape, jnp.bfloat16),
            pltpu.VMEM(field.shape, jnp.bfloat16),
            pltpu.SemaphoreType.DMA((steps,)),
            pltpu.SemaphoreType.DMA((1,)),
        ],
        compiler_params=pltpu.CompilerParams(vmem_limit_bytes=12 << 20),
        name="sweep",
    )(table, *tiles, noise, scale, *more)
    results = list(results)
    out = results.pop(0)
    front = results.pop(0) if part > 0 else None
    return out, front, results.pop(0) if results else None


def assemble_kernel(places, carries, *refs):
    count = len(places)
    refs = list(refs)
    carried = []
    if carries:
        carried.append(pltpu.make_async_copy(refs.pop(count), refs.pop(count + 2), refs[-1].at[count, 0]))
        carried[0].start()
    sems, pads = refs[-1], refs[-1 - count : -1]
    pieces, earlier, (target, table) = refs[:count], refs[count : -3 - count], refs[-3 - count : -1 - count]
    steps, span, size = target.shape[1:]
    copies = []
    for i, (q, s) in enumerate(places):
        blocks, some = pieces[i].shape[:2]
        copies.append(pltpu.make_async_copy(pieces[i].at[:, :, pl.ds(span - PAD, PAD)], pads[i], sems.at[i, 0]))
        copies.append(
            pltpu.make_async_copy(pieces[i], target.at[pl.ds(q, blocks), pl.ds(s, some)], sems.at[i, 1])
        )
    for copy in copies:
        copy.start()
    for copy in copies[::2]:
        copy.wait()
    per_line = size // ENTRY
    skip = earlier[0].shape[0] if earlier else 0
    if earlier:
        table[pl.ds(0, skip)] = earlier[0][...]
    where = {}
    for i, (q, s) in enumerate(places):
        for b in range(pads[i].shape[0]):
            for t in range(pads[i].shape[1]):
                where[(q + b) * steps + s + t] = pads[i], b, t
    for line in range(len(where) // per_line):
        value = jnp.zeros((1, size), jnp.float32)
        for j in range(per_line):
            buffer, b, t = where[line * per_line + j]
            entries = jnp.sum(buffer[b, t].astype(jnp.float32), axis=0, keepdims=True)
            value = value + (pltpu.roll(entries, j * ENTRY, 1) if j else entries)
        table[pl.ds(skip + line, 1)] = value.astype(jnp.int32)
    for copy in copies[1::2] + carried:
        copy.wait()


def assemble(pieces, places, blocks, steps, earlier=(), carry=()):
    anywhere = pl.BlockSpec(memory_space=pl.ANY)
    span, size = pieces[0].shape[2:]
    bytes_moved = sum(p.size * 4 for p in pieces)
    lines = blocks * steps * ENTRY // size + sum(e.shape[0] for e in earlier)
    vmem = pl.BlockSpec(memory_space=pltpu.VMEM)
    return pl.pallas_call(
        functools.partial(assemble_kernel, places, len(carry)),
        out_shape=(
            jax.ShapeDtypeStruct((blocks, steps, span, size), jnp.bfloat16),
            jax.ShapeDtypeStruct((lines, size), jnp.int32),
            *[jax.ShapeDtypeStruct(c.shape, c.dtype) for c in carry],
        ),
        in_specs=[anywhere] * (len(pieces) + len(carry)) + [vmem] * len(earlier),
        out_specs=(anywhere, vmem, *[anywhere] * len(carry)),
        scratch_shapes=[pltpu.VMEM((*p.shape[:2], PAD, size), p.dtype) for p in pieces]
        + [pltpu.SemaphoreType.DMA((len(pieces) + 1, 2))],
        compiler_params=pltpu.CompilerParams(vmem_limit_bytes=2 << 20),
        cost_estimate=pl.CostEstimate(flops=0, bytes_accessed=bytes_moved, transcendentals=0),
        name="assemble",
    )(*pieces, *carry, *earlier)


def moved(value, dx, dy):
    pairs = [
        (y * SIDE + x, (y + dy) % SIDE * SIDE + (x + dx) % SIDE) for y in range(SIDE) for x in range(SIDE)
    ]
    return lax.ppermute(value, "space", pairs)


def along(axis, by):
    return (by, 0) if axis == 0 else (0, by)


def ring_gather(block, first, second):
    low = moved(block, *along(first, 1))
    high = moved(block, *along(first, -1))
    far_low = moved(low[:, :1], *along(first, 1))
    far_high = moved(high[:, 1:], *along(first, -1))
    far = jnp.concatenate([far_low, far_high], axis=1)
    bundle = jnp.concatenate([block, low, high, far], axis=0)
    half = bundle.shape[0] // 2
    below = moved(bundle, *along(second, 1))
    above = moved(bundle, *along(second, -1))
    far_below = moved(below[:half], *along(second, 1))
    far_above = moved(above[half:], *along(second, -1))
    return (bundle, below, above), (far_below, far_above)


def prepare_kernel(columns, spot, source, late, early, tiles, sems):
    steps, local_rows, kt, size = tiles.shape[:4]
    half = steps // 2
    copies = [pltpu.make_async_copy(source.at[s], tiles.at[s], sems.at[s]) for s in range(steps)]
    for copy in reversed(copies):
        copy.start()
    lane = lax.broadcasted_iota(jnp.int32, (PAD, size), 1)
    first = lax.broadcasted_iota(jnp.int32, (PAD, size), 0) == 0
    for s in reversed(range(steps)):
        target, t = (late, s - half) if s >= half else (early, s)
        entries = [columns[s, r, k] for r in range(local_rows) for k in range(kt)] + [spot[0], spot[1]]
        value = jnp.zeros((PAD, size), jnp.int32)
        for i, entry in enumerate(entries):
            value = jnp.where(first & (lane == i), entry, value)
        copies[s].wait()
        for r in range(local_rows):
            for k in range(kt):
                target[0, t, pl.ds((r * kt + k) * size, size)] = tiles[s, r, k].T
        target[0, t, pl.ds(local_rows * kt * size, PAD)] = value.astype(jnp.float32).astype(jnp.bfloat16)


def prepare(tiles, columns, spot):
    steps, local_rows, kt, size = tiles.shape[:4]
    smem = pl.BlockSpec(memory_space=pltpu.SMEM)
    vmem = pl.BlockSpec(memory_space=pltpu.VMEM)
    shape = jax.ShapeDtypeStruct((1, steps // 2, local_rows * kt * size + PAD, size), jnp.bfloat16)
    return pl.pallas_call(
        prepare_kernel,
        out_shape=(shape, shape),
        in_specs=[smem, smem, pl.BlockSpec(memory_space=pl.ANY)],
        out_specs=(vmem, vmem),
        scratch_shapes=[pltpu.VMEM(tiles.shape, tiles.dtype), pltpu.SemaphoreType.DMA((steps,))],
        compiler_params=pltpu.CompilerParams(vmem_limit_bytes=16 << 20),
        name="prepare",
    )(columns, spot, pltpu.with_memory_space_constraint(tiles, pltpu.HBM))


def on_device(noise, scale, tiles, columns):
    steps, local_samples, node_count = noise.shape
    local_rows, kt, size = tiles.shape[1:4]
    parts = lax.axis_size("tm")
    spot = jnp.stack([lax.axis_index("space"), lax.axis_index("tm")]).astype(jnp.int32)
    half = steps // 2
    scale_rows = scale.reshape(steps, 1, node_count)

    span = local_rows * kt * size + PAD
    late, early = prepare(tiles, columns, spot)
    late_near, late_far = ring_gather(late, 0, 1)
    early_near, early_far = ring_gather(early, 1, 0)
    near, near_table, noise = assemble(
        [pltpu.with_memory_space_constraint(p, pltpu.HBM) for p in (*late_near, *early_near)],
        [(i * SIDE, s) for s in (half, 0) for i in range(3)],
        3 * SIDE,
        steps,
        carry=(noise,),
    )
    far, table = assemble(
        (*late_far, *early_far),
        [(i * SIDE // 2, s) for s in (half, 0) for i in range(2)],
        SIDE,
        steps,
        (near_table,),
    )
    table, full = table.reshape(-1), (near, far)

    out = tail = before = None
    fronts = [None] * BLOCKS
    for part in reversed(range(parts)):
        for block in range(BLOCKS):
            out, front, tail = sweep(
                table, full, noise, scale_rows, fronts[block], tail, out, part, block, before, kt, local_rows
            )
            before = (part, block)
            if part > 0:
                fronts[block] = lax.ppermute(front, "tm", [(part, part - 1)])
    return out


def solution(mesh):
    placed = (
        P("tm", "space", None),
        P("tm", None),
        P("tm", "space", None, None, None),
        P("tm", "space", None),
    )
    return jax.shard_map(
        on_device, mesh=mesh, in_specs=placed, out_specs=P("tm", "space", None), check_vma=False
    )
```

```python
import functools
import jax
import jax.numpy as jnp
from jax import lax
from jax.experimental import pallas as pl
from jax.experimental.pallas import tpu as pltpu
from jax.sharding import PartitionSpec as P

BLOCKS = 2
SIDE = 4
PAD = 16
ENTRY = 16


def sweep_kernel(part, block, before, first, ends, kt, local_rows, *refs):
    table, near, far, noise, scale = refs[:5]
    refs = list(refs[5:])
    front = None if first else refs.pop(0)
    tail = None if before is None else refs.pop(0)
    if before is not None:
        refs.pop(0)
    out = refs.pop(0)
    front_out, tail_out = (None, None) if ends else (refs.pop(0), None)
    if not (part == 0 and block == BLOCKS - 1):
        tail_out = refs.pop(0)
    out_buf, even, odd, out_sem, tail_sem = refs
    odd = odd if front_out is None else front_out
    steps, size = near.shape[1], near.shape[3]
    depth = kt * size
    width = even.shape[1]
    mine = pl.ds(block * width, width)
    here = table[local_rows * kt + 1]

    def out_copy(s):
        return pltpu.make_async_copy(out_buf.at[s], out.at[s, mine], out_sem.at[s])

    def flush(action):
        if before is not None:
            held = pl.ds(before[1] * width, width)

            @pl.when(here == before[0])
            def _flush():
                action(pltpu.make_async_copy(tail, out.at[0, held], tail_sem.at[0]))

    def one_step(i, carry):
        s = steps - 1 - i
        row, picked, weight = [], [], []
        for base, tiles in ((0, near), (near.shape[0], far)):
            for b in range(tiles.shape[0]):
                entry = ((base + b) * steps + s) * ENTRY
                for q in range(local_rows):
                    row.append(table[entry + local_rows * kt] * local_rows + q)
                    picked.append([even[table[entry + q * kt + k]] for k in range(kt)])
                    weight.append((tiles, b, q * depth))
        zero = jnp.zeros((width, size), jnp.bfloat16)

        def part_of(r, start, stop):
            tiles, b, base = weight[r]
            return tiles[b, s, base + start : base + stop]

        def product(left, right):
            return jnp.dot(left, right, preferred_element_type=jnp.float32)

        mixed = [None] * len(row)
        for r in range(0, len(row), 2):
            main = [
                product(jnp.concatenate(picked[r + j][:-1], axis=1), part_of(r + j, 0, depth - size))
                for j in range(2)
            ]
            last = product(
                jnp.concatenate(
                    [
                        jnp.concatenate([picked[r][-1], zero], axis=1),
                        jnp.concatenate([zero, picked[r + 1][-1]], axis=1),
                    ],
                    axis=0,
                ),
                jnp.concatenate([part_of(r, depth - size, depth), part_of(r + 1, depth - size, depth)], axis=0),
            )
            mixed[r] = main[0] + last[:width]
            mixed[r + 1] = main[1] + last[width:]
        for r, value in zip(row, mixed):
            lanes = pl.ds(pl.multiple_of(r * size, size), size)
            total = noise[s, mine, lanes].astype(jnp.float32) + value
            value = (scale[s, :, lanes] * total).astype(jnp.bfloat16)
            out_buf[s, :, lanes] = value
            odd[r] = value

        @pl.when(i < steps - 1)
        def _next():
            out_copy(s).start()
            even[...] = odd[...]

        return carry

    flush(lambda copy: copy.start())

    @pl.when(here == part)
    def _active():
        even[...] = jnp.zeros(even.shape, even.dtype) if first else front[...]
        lax.fori_loop(0, steps, one_step, 0)
        if tail_out is None:
            out_copy(0).start()
            out_copy(0).wait()
        else:
            tail_out[...] = out_buf[0]
        for s in range(1, steps):
            out_copy(s).wait()

    flush(lambda copy: copy.wait())


def sweep(table, tiles, noise, scale, front, tail, out, part, block, before, kt, local_rows):
    steps, size = tiles[0].shape[1], tiles[0].shape[3]
    node_count = noise.shape[-1]
    width = noise.shape[1] // BLOCKS
    field = jax.ShapeDtypeStruct((node_count // size, width, size), jnp.bfloat16)
    anywhere = pl.BlockSpec(memory_space=pl.ANY)
    smem = pl.BlockSpec(memory_space=pltpu.SMEM)
    vmem = pl.BlockSpec(memory_space=pltpu.VMEM)
    more = [value for value in (front, tail) if value is not None]
    specs = [smem, vmem, vmem, vmem, vmem] + [vmem] * len(more)
    aliases = {}
    if out is not None:
        aliases = {len(specs): 0}
        specs.append(anywhere)
        more.append(out)
    shapes, places = [jax.ShapeDtypeStruct(noise.shape, noise.dtype)], [anywhere]
    if part > 0:
        shapes.append(field)
        places.append(vmem)
    if part > 0 or block < BLOCKS - 1:
        shapes.append(jax.ShapeDtypeStruct((width, node_count), jnp.bfloat16))
        places.append(vmem)
    results = pl.pallas_call(
        functools.partial(sweep_kernel, part, block, before, front is None, part == 0, kt, local_rows),
        out_shape=tuple(shapes),
        in_specs=specs,
        out_specs=tuple(places),
        input_output_aliases=aliases,
        scratch_shapes=[
            pltpu.VMEM((steps, width, node_count), jnp.bfloat16),
            pltpu.VMEM(field.shape, jnp.bfloat16),
            pltpu.VMEM(field.shape, jnp.bfloat16),
            pltpu.SemaphoreType.DMA((steps,)),
            pltpu.SemaphoreType.DMA((1,)),
        ],
        compiler_params=pltpu.CompilerParams(vmem_limit_bytes=12 << 20),
        name="sweep",
    )(table, *tiles, noise, scale, *more)
    results = list(results)
    out = results.pop(0)
    front = results.pop(0) if part > 0 else None
    return out, front, results.pop(0) if results else None


def assemble_kernel(places, carries, *refs):
    count = len(places)
    refs = list(refs)
    carried = []
    if carries:
        carried.append(pltpu.make_async_copy(refs.pop(count), refs.pop(count + 2), refs[-1].at[count, 0]))
        carried[0].start()
    sems, pads = refs[-1], refs[-1 - count : -1]
    pieces, earlier, (target, table) = refs[:count], refs[count : -3 - count], refs[-3 - count : -1 - count]
    steps, span, size = target.shape[1:]
    copies = []
    for i, (q, s) in enumerate(places):
        blocks, some = pieces[i].shape[:2]
        copies.append(pltpu.make_async_copy(pieces[i].at[:, :, pl.ds(span - PAD, PAD)], pads[i], sems.at[i, 0]))
        copies.append(
            pltpu.make_async_copy(pieces[i], target.at[pl.ds(q, blocks), pl.ds(s, some)], sems.at[i, 1])
        )
    for copy in copies:
        copy.start()
    for copy in copies[::2]:
        copy.wait()
    per_line = size // ENTRY
    skip = earlier[0].shape[0] if earlier else 0
    if earlier:
        table[pl.ds(0, skip)] = earlier[0][...]
    where = {}
    for i, (q, s) in enumerate(places):
        for b in range(pads[i].shape[0]):
            for t in range(pads[i].shape[1]):
                where[(q + b) * steps + s + t] = pads[i], b, t
    for line in range(len(where) // per_line):
        value = jnp.zeros((1, size), jnp.float32)
        for j in range(per_line):
            buffer, b, t = where[line * per_line + j]
            entries = jnp.sum(buffer[b, t].astype(jnp.float32), axis=0, keepdims=True)
            value = value + (pltpu.roll(entries, j * ENTRY, 1) if j else entries)
        table[pl.ds(skip + line, 1)] = value.astype(jnp.int32)
    for copy in copies[1::2] + carried:
        copy.wait()


def assemble(pieces, places, blocks, steps, earlier=(), carry=()):
    anywhere = pl.BlockSpec(memory_space=pl.ANY)
    span, size = pieces[0].shape[2:]
    bytes_moved = sum(p.size * 4 for p in pieces)
    lines = blocks * steps * ENTRY // size + sum(e.shape[0] for e in earlier)
    vmem = pl.BlockSpec(memory_space=pltpu.VMEM)
    return pl.pallas_call(
        functools.partial(assemble_kernel, places, len(carry)),
        out_shape=(
            jax.ShapeDtypeStruct((blocks, steps, span, size), jnp.bfloat16),
            jax.ShapeDtypeStruct((lines, size), jnp.int32),
            *[jax.ShapeDtypeStruct(c.shape, c.dtype) for c in carry],
        ),
        in_specs=[anywhere] * (len(pieces) + len(carry)) + [vmem] * len(earlier),
        out_specs=(anywhere, vmem, *[anywhere] * len(carry)),
        scratch_shapes=[pltpu.VMEM((*p.shape[:2], PAD, size), p.dtype) for p in pieces]
        + [pltpu.SemaphoreType.DMA((len(pieces) + 1, 2))],
        compiler_params=pltpu.CompilerParams(vmem_limit_bytes=2 << 20),
        cost_estimate=pl.CostEstimate(flops=0, bytes_accessed=bytes_moved, transcendentals=0),
        name="assemble",
    )(*pieces, *carry, *earlier)


def moved(value, dx, dy):
    pairs = [
        (y * SIDE + x, (y + dy) % SIDE * SIDE + (x + dx) % SIDE) for y in range(SIDE) for x in range(SIDE)
    ]
    return lax.ppermute(value, "space", pairs)


def along(axis, by):
    return (by, 0) if axis == 0 else (0, by)


def ring_gather(block, first, second):
    low = moved(block, *along(first, 1))
    high = moved(block, *along(first, -1))
    far_low = moved(low[:, :1], *along(first, 1))
    far_high = moved(high[:, 1:], *along(first, -1))
    far = jnp.concatenate([far_low, far_high], axis=1)
    bundle = jnp.concatenate([block, low, high, far], axis=0)
    half = bundle.shape[0] // 2
    below = moved(bundle, *along(second, 1))
    above = moved(bundle, *along(second, -1))
    far_below = moved(below[:half], *along(second, 1))
    far_above = moved(above[half:], *along(second, -1))
    return (bundle, below, above), (far_below, far_above)


def prepare_kernel(columns, spot, source, late, early, tiles, sems):
    steps, local_rows, kt, size = tiles.shape[:4]
    half = steps // 2
    copies = [pltpu.make_async_copy(source.at[s], tiles.at[s], sems.at[s]) for s in range(steps)]
    for copy in reversed(copies):
        copy.start()
    lane = lax.broadcasted_iota(jnp.int32, (PAD, size), 1)
    first = lax.broadcasted_iota(jnp.int32, (PAD, size), 0) == 0
    for s in reversed(range(steps)):
        target, t = (late, s - half) if s >= half else (early, s)
        entries = [columns[s, r, k] for r in range(local_rows) for k in range(kt)] + [spot[0], spot[1]]
        value = jnp.zeros((PAD, size), jnp.int32)
        for i, entry in enumerate(entries):
            value = jnp.where(first & (lane == i), entry, value)
        copies[s].wait()
        for r in range(local_rows):
            for k in range(kt):
                target[0, t, pl.ds((r * kt + k) * size, size)] = tiles[s, r, k].T
        target[0, t, pl.ds(local_rows * kt * size, PAD)] = value.astype(jnp.float32).astype(jnp.bfloat16)


def prepare(tiles, columns, spot):
    steps, local_rows, kt, size = tiles.shape[:4]
    smem = pl.BlockSpec(memory_space=pltpu.SMEM)
    vmem = pl.BlockSpec(memory_space=pltpu.VMEM)
    shape = jax.ShapeDtypeStruct((1, steps // 2, local_rows * kt * size + PAD, size), jnp.bfloat16)
    return pl.pallas_call(
        prepare_kernel,
        out_shape=(shape, shape),
        in_specs=[smem, smem, pl.BlockSpec(memory_space=pl.ANY)],
        out_specs=(vmem, vmem),
        scratch_shapes=[pltpu.VMEM(tiles.shape, tiles.dtype), pltpu.SemaphoreType.DMA((steps,))],
        compiler_params=pltpu.CompilerParams(vmem_limit_bytes=16 << 20),
        name="prepare",
    )(columns, spot, pltpu.with_memory_space_constraint(tiles, pltpu.HBM))


def on_device(noise, scale, tiles, columns):
    steps, local_samples, node_count = noise.shape
    local_rows, kt, size = tiles.shape[1:4]
    parts = lax.axis_size("tm")
    spot = jnp.stack([lax.axis_index("space"), lax.axis_index("tm")]).astype(jnp.int32)
    half = steps // 2
    scale_rows = scale.reshape(steps, 1, node_count)

    span = local_rows * kt * size + PAD
    late, early = prepare(tiles, columns, spot)
    late_near, late_far = ring_gather(late, 0, 1)
    early_near, early_far = ring_gather(early, 1, 0)
    near, near_table, noise = assemble(
        [pltpu.with_memory_space_constraint(p, pltpu.HBM) for p in (*late_near, *early_near)],
        [(i * SIDE, s) for s in (half, 0) for i in range(3)],
        3 * SIDE,
        steps,
        carry=(noise,),
    )
    far, table = assemble(
        (*late_far, *early_far),
        [(i * SIDE // 2, s) for s in (half, 0) for i in range(2)],
        SIDE,
        steps,
        (near_table,),
    )
    table, full = table.reshape(-1), (near, far)

    out = tail = before = None
    fronts = [None] * BLOCKS
    for part in reversed(range(parts)):
        for block in range(BLOCKS):
            out, front, tail = sweep(
                table, full, noise, scale_rows, fronts[block], tail, out, part, block, before, kt, local_rows
            )
            before = (part, block)
            if part > 0:
                fronts[block] = lax.ppermute(front, "tm", [(part, part - 1)])
    return out


def solution(mesh):
    placed = (
        P("tm", "space", None),
        P("tm", None),
        P("tm", "space", None, None, None),
        P("tm", "space", None),
    )
    return jax.shard_map(
        on_device, mesh=mesh, in_specs=placed, out_specs=P("tm", "space", None), check_vma=False
    )
```
